32 devices in a mesh: frame: 2 (over x), tile: 16 (over z, y, core).
Axes of the slice: x: 2, y: 2, z: 4, core: 2. Of those that a mesh axis runs over, the one named last changes fastest.
Arguments:
- latents: bfloat16 [4, 64, 128, 512], P('frame', 'tile'), may hold values from -6 to 6
- conv_weight: bfloat16 [3, 3, 512, 512], replicated, may hold values from -0.09375 to 0.09375
- conv_bias: float32 [512], replicated, may hold values from -3 to 3
- query_weight: bfloat16 [512, 512], replicated, may hold values from -0.176776695 to 0.176776695
- key_weight: bfloat16 [512, 512], replicated, may hold values from -8 to 8
- value_weight: bfloat16 [512, 512], replicated, may hold values from -0.25 to 0.25
- out_weight: bfloat16 [512, 512], replicated, may hold values from -0.25 to 0.25
- cotangent: bfloat16 [4, 64, 128, 512], P('frame', 'tile'), may hold values from -0.032958984 to 0.032958984
Outputs:
- mixed_frames: bfloat16 [4, 64, 128, 512], P('frame', 'tile')
- conv_grad: float32 [512, 4608], P('tile', 'frame')
The draws below stay inside these ranges and needn't reach their ends.
All inputs are finite; a program needn't handle non-finite values.
Results may differ from the reference program's by a relative error of at most 0.0065.
Values may be sent and summed in bfloat16 or wider, within the bound.
A program may use at most 128 MiB of HBM per device.

```python
import math
import jax
import jax.numpy as jnp
from jax import lax

C = 512
HEADS = 8
COLS = 128
FRAMES = 4
HEIGHT = 64


def shared_pair(key):
    base = jnp.clip(jax.random.normal(jax.random.fold_in(key, 11), (C, C), jnp.float32), -4.0, 4.0) / math.sqrt(C)
    other = jnp.clip(jax.random.normal(jax.random.fold_in(key, 12), (C, C), jnp.float32), -4.0, 4.0) / math.sqrt(C)
    return (base, other)


def draw_query_weight(key, part):
    base, other = shared_pair(key)
    return base.astype(jnp.bfloat16)


def draw_key_weight(key, part):
    base, other = shared_pair(key)
    result = other
    return result.astype(jnp.bfloat16)


def spiked(array, rng, source, target, blocks, factor):
    def block_of(position):
        return (jnp.arange(array.shape[position]) // (array.shape[position] // blocks)).reshape((-1,) + (1,) * (array.ndim - 1 - position))

    one_side = jax.random.permutation(rng, blocks)[block_of(target)]
    far = (block_of(target) + blocks // 2) % blocks
    return jnp.where((block_of(source) == one_side) | (block_of(source) == far), factor * array, array)


def level_of(rng, extent, shards, least, largest):
    def one(dim, shards_of):
        heights = jax.random.uniform(jax.random.fold_in(jax.random.fold_in(rng, 6), dim), (shards_of,), jnp.float32, least / len(shards), largest / len(shards))
        return jnp.repeat(jnp.exp(heights), extent[dim] // shards_of).reshape((-1,) + (1,) * (len(extent) - dim - 1))

    loudness = one(*shards[0])
    for cut in shards[1:]:
        loudness = loudness * one(*cut)
    return loudness


def centred(stream_key, extent, spread, most, shards=(), dtype=jnp.bfloat16):
    gain = level_of(stream_key, extent, shards, -0.22, 0.18) if shards else 1.0
    drawn = jax.random.normal(stream_key, extent, jnp.float32) * spread * gain
    return jnp.minimum(jnp.maximum(drawn, -most), most).astype(dtype)


def gaussian_with(key, extent, spread, reach, cuts, heavy, kind=jnp.bfloat16):
    drawn = spread * jax.random.normal(key, extent, jnp.float32)
    if cuts:
        drawn = drawn * level_of(key, extent, cuts, -0.22, 0.18)
    return jnp.clip(spiked(drawn, jax.random.fold_in(key, 3), *heavy), -reach, reach).astype(kind)


def setup_inputs(seed: int = 0) -> dict:
    key_list = jax.random.split(jax.random.key(seed), 9)
    latents = centred(key_list[0], (FRAMES, HEIGHT, COLS, C), 1.0, 6.0, ((0, 2), (1, 16)))
    conv_weight = centred(key_list[1], (3, 3, C, C), (9 * C) ** -0.5, 0.09375)
    conv_bias = centred(key_list[2], (C,), 0.5, 3.0, (), jnp.float32)
    query_weight = draw_query_weight(jax.random.fold_in(key_list[8], 71), 0)
    key_weight = draw_key_weight(jax.random.fold_in(key_list[8], 71), 0)
    value_weight = centred(key_list[5], (C, C), C ** -0.5, 0.25)
    out_weight = centred(key_list[6], (C, C), C ** -0.5, 0.25)
    cotangent = gaussian_with(key_list[7], (FRAMES, HEIGHT, COLS, C), ((FRAMES * HEIGHT * COLS) ** -0.5), 0.032958984, ((0, 2), (1, 16)), (1, 3, 16, 2.0))
    return dict(latents=latents, conv_weight=conv_weight, conv_bias=conv_bias, query_weight=query_weight, key_weight=key_weight, value_weight=value_weight, out_weight=out_weight, cotangent=cotangent)


def attention(hidden, query_weight, key_weight, value_weight, out_weight):
    frames, height, cols, channels = hidden.shape
    head_dim = channels // HEADS
    tokens = hidden.astype(jnp.float32).reshape(-1, channels)
    queries = jnp.dot(tokens, query_weight.astype(jnp.float32), precision=lax.Precision.HIGHEST).astype(jnp.bfloat16)
    key_rows = jnp.dot(tokens, key_weight.astype(jnp.float32), precision=lax.Precision.HIGHEST).astype(jnp.bfloat16)
    values = jnp.dot(tokens, value_weight.astype(jnp.float32), precision=lax.Precision.HIGHEST).astype(jnp.bfloat16)
    shaped = (frames, height * cols, HEADS, head_dim)
    queries = queries.astype(jnp.float32).reshape(shaped)
    key_rows = key_rows.astype(jnp.float32).reshape(shaped)
    values = values.astype(jnp.float32).reshape(shaped)
    scores = jnp.einsum('fphd,gphd->phfg', queries, key_rows, precision=lax.Precision.HIGHEST) / math.sqrt(head_dim)
    weights = jax.nn.softmax(scores, axis=-1).astype(jnp.bfloat16).astype(jnp.float32)
    head_out = jnp.einsum('phfg,gphd->fphd', weights, values, precision=lax.Precision.HIGHEST).astype(jnp.bfloat16)
    projected = jnp.dot(head_out.astype(jnp.float32).reshape(-1, channels), out_weight.astype(jnp.float32), precision=lax.Precision.HIGHEST)
    mixed = tokens + projected
    return mixed.astype(jnp.bfloat16).reshape(frames, height, cols, channels)

def reference(latents, conv_weight, conv_bias, query_weight, key_weight, value_weight, out_weight, cotangent):
    convolved = lax.conv_general_dilated(latents.astype(jnp.float32), conv_weight.astype(jnp.float32), (1, 1), ((1, 1), (1, 1)), dimension_numbers=('NHWC', 'HWIO', 'NHWC'), precision=lax.Precision.HIGHEST)
    hidden = jax.nn.silu(convolved + conv_bias).astype(jnp.bfloat16)
    mixed_frames = attention(hidden, query_weight, key_weight, value_weight, out_weight)
    frames, height, cols, channels = mixed_frames.shape
    padded = jnp.pad(mixed_frames.astype(jnp.float32), ((0, 0), (1, 1), (1, 1), (0, 0)))
    flat_cot = cotangent.astype(jnp.float32).reshape(-1, channels)
    pieces = []
    for row_shift in range(3):
        for col_shift in range(3):
            shifted = padded[:, row_shift:row_shift + height, col_shift:col_shift + cols, :].reshape(-1, channels)
            pieces.append(lax.dot_general(flat_cot, shifted, (((0,), (0,)), ((), ())), precision=lax.Precision.HIGHEST))
    conv_grad = jnp.concatenate(pieces, axis=1)
    return (mixed_frames, conv_grad)
```

```python
import functools
import math

import jax
import jax.numpy as jnp
from jax import lax
from jax.experimental import pallas as pl
from jax.experimental.pallas import tpu as pltpu
from jax.sharding import PartitionSpec as P

HEADS = 8
LANES = 128
GROUP = 2
PIECES = 2
MESH = pl.DeviceIdType.MESH
F32 = jnp.float32
BF16 = jnp.bfloat16


def bit_count(size):
    return size.bit_length() - 1


PATHS = (
    "zmyx", "yzmx", "zmxy", "xzym", "yxzm", "yxzm", "xyzm", "zxym", "xyzm",
)
PLAN = (
    (0, -1), (1, -1), (2, -1), (3, -1), (4, -1), (6, -1), (5, -1), (7, -1), (8, -1),
    (0, 0), (1, 0), (2, 0), (3, 0), (4, 0), (6, 0), (5, 0), (8, 0), (6, 1),
    (4, 1), (7, 0), (1, 1), (3, 1), (5, 1), (0, 1), (8, 1), (6, 2), (2, 1),
    (4, 2), (7, 1), (3, 2), (5, 2), (1, 2), (0, 2), (8, 2), (2, 2), (6, 3),
    (4, 3), (7, 2), (1, 3), (0, 3), (2, 3), (3, 3), (5, 3), (8, 3), (7, 3),
)


def orders_of(frames_n, tiles_n):
    tile_bits = [("tile", b) for b in range(bit_count(GROUP), bit_count(tiles_n))]
    kinds = {
        "x": [("frame", b) for b in range(bit_count(frames_n))],
        "y": tile_bits[:1],
        "z": tile_bits[1:2],
        "m": tile_bits[2:],
    }
    return [sum((kinds[kind] for kind in path), []) for path in PATHS]


def plan_of(chunks, halvings):
    if chunks == len(PATHS) and halvings == len(PATHS[0]):
        return PLAN
    return [(k, stage) for stage in range(-1, halvings) for k in range(chunks)]


def attend(queries, keys, values, own, wo, same_head):
    pixels, channels = queries[0].shape
    groups = channels // LANES
    scale = 1.0 / math.sqrt(channels // HEADS)
    heads_out = []
    for q in queries:
        wide = q.astype(F32)
        folded = []
        for k in keys:
            product = wide * k.astype(F32)
            total = product[:, :LANES]
            for c in range(1, groups):
                total = total + product[:, c * LANES : (c + 1) * LANES]
            high = total.astype(BF16)
            low = (total - high.astype(F32)).astype(BF16)
            folded.append(jnp.concatenate([high, low], axis=1))
        scores = jnp.dot(jnp.concatenate(folded, axis=0), same_head, preferred_element_type=F32)
        scores = [scores[g * pixels : (g + 1) * pixels] * scale for g in range(len(keys))]
        top = functools.reduce(jnp.maximum, scores)
        exps = [jnp.exp(s - top) for s in scores]
        share = 1.0 / functools.reduce(jnp.add, exps)
        acc = [None] * groups
        for e, v in zip(exps, values):
            weight = (e * share).astype(BF16).astype(F32)
            for c in range(groups):
                term = weight * v[:, c * LANES : (c + 1) * LANES].astype(F32)
                acc[c] = term if acc[c] is None else acc[c] + term
        heads_out.append(jnp.concatenate(acc, axis=1).astype(BF16))
    projected = jnp.dot(jnp.concatenate(heads_out, axis=0), wo, preferred_element_type=F32)
    return (own.astype(F32) + projected).astype(BF16)


def block_kernel(
    lat_hbm, conv_hbm, bias_ref, wq_hbm, wk_hbm, wv_hbm, wo_hbm, cot_hbm,
    mixed_hbm, grad_ref,
    lat_ref, conv_ref, weights, cot_ref, lat_rim, moved, hidden, others, queries, keys, values,
    turned, gathered, shifted, mixed_all, acc, part, recv,
    load_sem, conv_sem, own_sem, store_sem, rim_send, rim_recv, hid_send, hid_recv,
    cot_send, cot_recv, edge_send, edge_recv, mix_send, mix_recv, red_send, red_recv,
):
    frames, rows, cols, channels = lat_hbm.shape
    side = conv_hbm.shape[0]
    count, tiles = lax.axis_size("frame"), lax.axis_size("tile")
    frame, tile = lax.axis_index("frame"), lax.axis_index("tile")
    depth = tiles // GROUP
    block_rows = turned.shape[3]
    outs = depth * block_rows
    strip, member = tile // GROUP, lax.rem(tile, GROUP)
    has = (tile > 0, tile < tiles - 1)
    width = channels // count
    chunks, blocks = part.shape[0], part.shape[1]
    piece_cols = cols // PIECES

    squares = (wq_hbm, wk_hbm, wv_hbm, wo_hbm)
    lat_load = pltpu.make_async_copy(lat_hbm, lat_ref, load_sem.at[0])
    cot_load = pltpu.make_async_copy(cot_hbm, cot_ref, load_sem.at[1])
    conv_loads = [
        [pltpu.make_async_copy(conv_hbm.at[r, s], conv_ref.at[r, s], conv_sem.at[r, s]) for s in range(side)]
        for r in range(side)
    ]
    square_loads = [
        pltpu.make_async_copy(source, weights.at[j], load_sem.at[2 + j])
        for j, source in enumerate(squares)
    ]
    for load in [lat_load] + sum(conv_loads, []) + [cot_load] + square_loads:
        load.start()

    def flip(axis, b):
        here = {"tile": tile, "frame": frame}[axis]
        return {axis: here + (1 - 2 * lax.rem(here // (1 << b), 2)) * (1 << b)}

    barrier = pltpu.get_barrier_semaphore()

    def greet(friend):
        pl.semaphore_signal(barrier, inc=1, device_id=friend, device_id_type=MESH)

    for k in range(1, GROUP + 1):

        @pl.when(tile >= k)
        def _():
            greet({"tile": tile - k})

        @pl.when(tile < tiles - k)
        def _():
            greet({"tile": tile + k})

    greeted = [flip("tile", b) for b in range(bit_count(GROUP) + 1, bit_count(tiles))]
    greeted += [{"frame": lax.rem(frame + k, count)} for k in range(1, count)]
    for friend in greeted:
        greet(friend)
    expected = jnp.minimum(tile, GROUP) + jnp.minimum(tiles - 1 - tile, GROUP) + len(greeted)

    def rim_copy(end, landed):
        return pltpu.make_async_remote_copy(
            src_ref=lat_hbm.at[:, (rows - 1) * end],
            dst_ref=lat_rim.at[end if landed else 1 - end],
            send_sem=rim_send.at[end],
            recv_sem=rim_recv.at[end if landed else 1 - end],
            device_id={"tile": tile + (1 if end else -1)},
            device_id_type=MESH,
        )

    def by_lead(value, offset, axis):
        if offset == 0:
            return value
        wide = value.astype(F32)
        rolled = pltpu.roll(wide, (-offset) % cols, axis)
        at = lax.broadcasted_iota(jnp.int32, wide.shape, axis)
        edge = 0 if offset < 0 else cols - 1
        return jnp.where(at == edge, 0.0, rolled).astype(BF16)

    def place(value, f, row):
        for s in range(side):
            moved[s, f, row] = by_lead(value, s - 1, 0)

    def cot_copy(k, landed):
        other = lax.rem(member + (GROUP - k if landed else k), GROUP)
        sender = other if landed else member
        return pltpu.make_async_remote_copy(
            src_ref=turned.at[:, :, other],
            dst_ref=gathered.at[:, :, :, pl.ds(pl.multiple_of(cols + sender * (rows * cols), LANES), rows * cols)],
            send_sem=cot_send.at[k - 1],
            recv_sem=cot_recv.at[k - 1],
            device_id={"tile": strip * GROUP + other},
            device_id_type=MESH,
        )

    def edge_copy(end, m):
        first = (rows - 1) * cols if end else 0
        target = 0 if end else (GROUP * rows + 1) * cols
        return pltpu.make_async_remote_copy(
            src_ref=turned.at[:, :, m, :, pl.ds(first, cols)],
            dst_ref=gathered.at[:, :, :, pl.ds(target, cols)],
            send_sem=edge_send.at[end, m],
            recv_sem=edge_recv.at[end],
            device_id={"tile": (strip + (1 if end else -1)) * GROUP + m},
            device_id_type=MESH,
        )

    edge_sends = (
        jnp.logical_and(member == 0, strip > 0),
        jnp.logical_and(member == GROUP - 1, strip < depth - 1),
    )
    own_cot = pltpu.make_async_copy(
        turned.at[:, :, member],
        gathered.at[:, :, :, pl.ds(pl.multiple_of(cols + member * (rows * cols), LANES), rows * cols)],
        own_sem.at[0],
    )
    lat_load.wait()
    for row in range(rows):
        for f in range(frames):
            place(lat_ref[f, row], f, row + 1)

    pl.semaphore_wait(barrier, expected)
    for end in range(2):

        @pl.when(has[end])
        def _():
            rim_copy(end, False).start()

    def hidden_copy(k, row, h):
        span = pl.ds(h * piece_cols, piece_cols)
        return pltpu.make_async_remote_copy(
            src_ref=hidden.at[row, :, span],
            dst_ref=others.at[k - 1, row, :, span],
            send_sem=hid_send.at[k - 1, row, h],
            recv_sem=hid_recv.at[k - 1, row, h],
            device_id={"frame": lax.rem(frame + k, count)},
            device_id_type=MESH,
        )

    def convolve(row, first):
        total = jnp.broadcast_to(bias_ref[...], (frames * cols, channels))
        for r in range(side):
            for s in range(side):
                if first:
                    conv_loads[r][s].wait()
                total = total + jnp.dot(
                    moved[s, :, row + r].reshape(frames * cols, channels),
                    conv_ref[r, s],
                    preferred_element_type=F32,
                )
        result = total / (1.0 + jnp.exp(-total))
        hidden[row] = result.astype(BF16).reshape(frames, cols, channels)

    order = list(range(1, rows - 1)) + [rows - 1, 0]
    units = [(row, h) for row in order for h in range(PIECES)]

    def release(n):
        for k in range(1, count):
            hidden_copy(k, *units[n]).start()

    for n, row in enumerate(order[: rows - 2]):
        convolve(row, n == 0)
        release(2 * n)
        release(2 * n + 1)

    for load in square_loads:
        load.wait()
    head_dim = channels // HEADS
    i = lax.broadcasted_iota(jnp.int32, (channels, channels), 0)
    j = lax.broadcasted_iota(jnp.int32, (channels, channels), 1)
    spread = (i == lax.rem(j, HEADS) * head_dim + j // HEADS).astype(F32).astype(BF16)
    collect = (j == lax.rem(i, HEADS) * head_dim + i // HEADS).astype(F32).astype(BF16)
    for n in range(3):
        weights[n] = jnp.dot(weights[n], spread, preferred_element_type=F32).astype(BF16)
    weights[3] = jnp.dot(collect, weights[3], preferred_element_type=F32).astype(BF16)
    def project(row):
        tokens = hidden[row].reshape(frames * cols, channels)
        for n, target in enumerate((queries, keys, values)):
            result = jnp.dot(tokens, weights[n], preferred_element_type=F32)
            target[row] = result.astype(BF16).reshape(frames, cols, channels)

    for row in order[: rows - 2]:
        project(row)
    cot_load.wait()
    for f in range(frames):
        for row in range(rows):
            upright = cot_ref[f, row].T
            for d in range(depth):
                for m in range(GROUP):
                    at = (d * GROUP + m) * block_rows
                    turned[f, d, m, :, row * cols : (row + 1) * cols] = upright[at : at + block_rows]
    own_cot.start()
    for k in range(1, GROUP):
        cot_copy(k, False).start()
    for end in range(2):

        @pl.when(edge_sends[end])
        def _():
            for m in range(GROUP):
                edge_copy(end, m).start()

    for end in range(2):

        @pl.when(has[end])
        def _():
            rim_copy(end, True).wait_recv()

        @pl.when(jnp.logical_not(has[end]))
        def _():
            lat_rim[end] = jnp.zeros_like(lat_rim[end])

    for f in range(frames):
        place(lat_rim[0, f], f, 0)
        place(lat_rim[1, f], f, rows + 1)
    for row in order[rows - 2 :]:
        convolve(row, False)
    released = 2 * (rows - 2) + 1
    release(released - 1)
    for row in order[rows - 2 :]:
        project(row)

    own_cot.wait()
    for k in range(1, GROUP):
        cot_copy(k, True).wait_recv()
    rims = (strip > 0, strip < depth - 1)
    for end in range(2):
        target = 0 if end == 0 else (GROUP * rows + 1) * cols

        @pl.when(rims[end])
        def _():
            edge_copy(1 - end, 0).wait_recv()

        @pl.when(jnp.logical_not(rims[end]))
        def _():
            gathered[:, :, :, target : target + cols] = jnp.zeros(
                (frames, depth, block_rows, cols), BF16
            )

    for f in range(frames):
        for q in range(GROUP * rows + 2):
            value = gathered[f, :, :, q * cols : (q + 1) * cols].reshape(outs, cols)
            for s in range(side):
                shifted[f, s * outs : (s + 1) * outs, q * cols : (q + 1) * cols] = by_lead(value, 1 - s, 1)

    lane_i = lax.broadcasted_iota(jnp.int32, (2 * LANES, LANES), 0)
    lane_j = lax.broadcasted_iota(jnp.int32, (2 * LANES, LANES), 1)
    same_head = (lax.rem(lane_i, HEADS) == lax.rem(lane_j, HEADS)).astype(F32).astype(BF16)

    def mix_copy(row, h, landed):
        span = pl.ds(h * piece_cols, piece_cols)
        at = 1 - member if landed else member
        return pltpu.make_async_remote_copy(
            src_ref=mixed_all.at[row, member, :, span],
            dst_ref=mixed_all.at[row, at, :, span],
            send_sem=mix_send.at[row, h],
            recv_sem=mix_recv.at[row, h],
            device_id={"tile": strip * GROUP + 1 - member},
            device_id_type=MESH,
        )

    def attend_piece(row, h, following):
        span = pl.ds(h * piece_cols, piece_cols)
        for k in range(1, count):
            hidden_copy(k, row, h).wait_recv()
        if released <= following < len(units):
            release(following)
        own_k, own_v = [], []
        for f in range(frames):
            own_k.append(keys[row, f, span])
            own_v.append(values[row, f, span])
        for k in range(1, count):
            tokens = others[k - 1, row, :, span].reshape(frames * piece_cols, channels)
            kk = jnp.dot(tokens, weights[1], preferred_element_type=F32).astype(BF16)
            vv = jnp.dot(tokens, weights[2], preferred_element_type=F32).astype(BF16)
            for f in range(frames):
                own_k.append(kk[f * piece_cols : (f + 1) * piece_cols])
                own_v.append(vv[f * piece_cols : (f + 1) * piece_cols])
        mixed = attend(
            [queries[row, f, span] for f in range(frames)], own_k, own_v,
            hidden[row, :, span].reshape(frames * piece_cols, channels), weights[3], same_head,
        )
        mixed_all[row, member, :, span] = mixed.reshape(frames, piece_cols, channels)
        mix_copy(row, h, False).start()

    def store(row):
        return pltpu.make_async_copy(
            mixed_all.at[row, member], mixed_hbm.at[:, pl.ds(row * cols, cols)], store_sem.at[row]
        )

    def accumulate(row, first):
        for h in range(PIECES):
            mix_copy(row, h, True).wait_recv()
        maps = mixed_all[row].reshape(GROUP * frames * cols, channels)
        for r in range(side):
            taps = []
            for m in range(GROUP):
                lo = (m * rows + row + side - 1 - r) * cols
                for f in range(frames):
                    taps.append(shifted[f, :, lo : lo + cols])
            term = jnp.dot(jnp.concatenate(taps, axis=1), maps, preferred_element_type=F32)
            acc[r] = term if first else acc[r] + term

    for n, (row, h) in enumerate(units):
        attend_piece(row, h, n + 3)
        if h == PIECES - 1:
            store(row).start()
        if n >= PIECES + 1 and h == 1 % PIECES:
            accumulate(units[n - PIECES][0], n - PIECES < PIECES)
    accumulate(units[-1][0], len(units) == PIECES)

    orders = orders_of(count, tiles)
    halvings = len(orders[0])
    here = {"tile": tile, "frame": frame}

    def my_bit(axis, b):
        return lax.rem(here[axis] // (1 << b), 2)

    def order_of(k):
        return orders[k % len(orders)]

    def start_of(k, stage):
        total = 0
        for j in range(stage):
            total = total + my_bit(*order_of(k)[j]) * (blocks >> (j + 1))
        return total

    def sum_copy(k, stage):
        axis, b = order_of(k)[stage]
        size = blocks >> (stage + 1)
        source = start_of(k, stage) + (1 - my_bit(axis, b)) * size
        return pltpu.make_async_remote_copy(
            src_ref=part.at[k, pl.ds(source, size)],
            dst_ref=recv.at[k, pl.ds(size, size)],
            send_sem=red_send.at[k, stage],
            recv_sem=red_recv.at[k, stage],
            device_id=flip(axis, b),
            device_id_type=MESH,
        )

    def cut(k):
        for f in range(count):
            unit = f * chunks + k
            tap, col = (unit * width) // channels, (unit * width) % channels
            r, s = tap // side, tap % side
            for d in range(depth):
                at = {"tile": d * GROUP, "frame": f}
                place_at = 0
                for j, (axis, b) in enumerate(order_of(k)):
                    place_at += ((at[axis] >> b) & 1) * (blocks >> (j + 1))
                lo = s * outs + d * block_rows
                part[k, place_at] = acc[r, lo : lo + block_rows, col : col + width].astype(BF16)
        sum_copy(k, 0).start()

    def merge(k, stage):
        sum_copy(k, stage).wait_recv()
        size = blocks >> (stage + 1)
        mine = start_of(k, stage + 1)
        total = part[k, pl.ds(mine, size)].astype(F32) + recv[k, size : 2 * size].astype(F32)
        if stage < halvings - 1:
            part[k, pl.ds(mine, size)] = total.astype(BF16)
            sum_copy(k, stage + 1).start()
        else:
            grad_ref[:, k * width : (k + 1) * width] = total[0]

    for k, stage in plan_of(chunks, halvings):
        if stage < 0:
            cut(k)
        else:
            merge(k, stage)

    for k in range(chunks):
        for stage in range(halvings):
            sum_copy(k, stage).wait_send()
    for row, h in units:
        mix_copy(row, h, False).wait_send()
        for k in range(1, count):
            hidden_copy(k, row, h).wait_send()
    for row in range(rows):
        store(row).wait()
    for k in range(1, GROUP):
        cot_copy(k, False).wait_send()
    for end in range(2):

        @pl.when(has[end])
        def _():
            rim_copy(end, False).wait_send()

        @pl.when(edge_sends[end])
        def _():
            for m in range(GROUP):
                edge_copy(end, m).wait_send()


def block(latents, conv_weight, conv_bias, wq, wk, wv, wo, cotangent):
    frames, rows, cols, channels = latents.shape
    side = conv_weight.shape[0]
    out_channels = cotangent.shape[3]
    count, tiles = lax.axis_size("frame"), lax.axis_size("tile")
    chunks, width = side * side, channels // count
    depth, block_rows = tiles // GROUP, out_channels // tiles
    outs, blocks = depth * block_rows, count * depth
    stages = len(orders_of(count, tiles)[0])
    hbm = pl.BlockSpec(memory_space=pltpu.HBM)
    vmem = pl.BlockSpec(memory_space=pltpu.VMEM)
    maps = (rows, frames, cols, channels)
    dma = pltpu.SemaphoreType.DMA
    return pl.pallas_call(
        block_kernel,
        out_shape=[
            jax.ShapeDtypeStruct((frames, rows * cols, channels), BF16),
            jax.ShapeDtypeStruct((block_rows, chunks * width), F32),
        ],
        in_specs=[hbm, hbm, vmem] + [hbm] * 5,
        out_specs=[hbm, vmem],
        scratch_shapes=[
            pltpu.VMEM(latents.shape, BF16),
            pltpu.VMEM(conv_weight.shape, BF16),
            pltpu.VMEM((4, channels, channels), BF16),
            pltpu.VMEM(cotangent.shape, BF16),
            pltpu.VMEM((2, frames, cols, channels), BF16),
            pltpu.VMEM((side, frames, rows + 2, cols, channels), BF16),
            pltpu.VMEM(maps, BF16),
            pltpu.VMEM((count - 1,) + maps, BF16),
            pltpu.VMEM(maps, BF16),
            pltpu.VMEM(maps, BF16),
            pltpu.VMEM(maps, BF16),
            pltpu.VMEM((frames, depth, GROUP, block_rows, rows * cols), BF16),
            pltpu.VMEM((frames, depth, block_rows, (GROUP * rows + 2) * cols), BF16),
            pltpu.VMEM((frames, side * outs, (GROUP * rows + 2) * cols), BF16),
            pltpu.VMEM((rows, GROUP, frames, cols, channels), BF16),
            pltpu.VMEM((side, side * outs, channels), F32),
            pltpu.VMEM((chunks, blocks, block_rows, width), BF16),
            pltpu.VMEM((chunks, blocks, block_rows, width), BF16),
            dma((6,)),
            dma((side, side)),
            dma((1,)),
            dma((rows,)),
            dma((2,)),
            dma((2,)),
            dma((count - 1, rows, PIECES)),
            dma((count - 1, rows, PIECES)),
            dma((GROUP - 1,)),
            dma((GROUP - 1,)),
            dma((2, GROUP)),
            dma((2,)),
            dma((rows, PIECES)),
            dma((rows, PIECES)),
            dma((chunks, stages)),
            dma((chunks, stages)),
        ],
        compiler_params=pltpu.CompilerParams(
            collective_id=0, has_side_effects=True, vmem_limit_bytes=63 * 1024 * 1024
        ),
    )(latents, conv_weight, conv_bias.reshape(1, -1), wq, wk, wv, wo, cotangent)


def settle_kernel(mixed_in, grad_in, mixed_out, grad_out, mixed_held, grad_held, in_sem, out_sem):
    half = mixed_in.shape[1] // 2
    parts = [(grad_in, grad_held, grad_out)]
    for f in range(mixed_in.shape[0]):
        for h in range(2):
            at = (f, pl.ds(h * half, half))
            parts.append((mixed_in.at[at], mixed_held.at[at], mixed_out.at[at]))
    inward = [pltpu.make_async_copy(a, b, in_sem.at[n]) for n, (a, b, _) in enumerate(parts)]
    outward = [pltpu.make_async_copy(b, c, out_sem.at[n]) for n, (_, b, c) in enumerate(parts)]
    for copy in inward:
        copy.start()
    for first, second in zip(inward, outward):
        first.wait()
        second.start()
    for copy in outward:
        copy.wait()


def settled(mixed, grad):
    hbm = pl.BlockSpec(memory_space=pltpu.HBM)
    parts = 1 + 2 * mixed.shape[0]
    return pl.pallas_call(
        settle_kernel,
        out_shape=[
            jax.ShapeDtypeStruct(mixed.shape, mixed.dtype),
            jax.ShapeDtypeStruct(grad.shape, grad.dtype),
        ],
        in_specs=[hbm, hbm],
        out_specs=[hbm, hbm],
        scratch_shapes=[
            pltpu.VMEM(mixed.shape, mixed.dtype),
            pltpu.VMEM(grad.shape, grad.dtype),
            pltpu.SemaphoreType.DMA((parts,)),
            pltpu.SemaphoreType.DMA((parts,)),
        ],
    )(mixed, grad)


def on_device(
    latents, conv_weight, conv_bias, query_weight, key_weight, value_weight, out_weight, cotangent
):
    frames, rows, cols, channels = latents.shape
    mixed, conv_grad = settled(
        *block(
            latents, conv_weight, conv_bias, query_weight, key_weight, value_weight, out_weight, cotangent
        )
    )
    return (mixed.reshape(frames, rows, cols, channels), conv_grad)


def solution(mesh):
    in_specs = (
        P("frame", "tile", None, None),
        P(),
        P(),
        P(),
        P(),
        P(),
        P(),
        P("frame", "tile", None, None),
    )
    out_specs = (P("frame", "tile", None, None), P("tile", "frame"))
    return jax.shard_map(
        on_device, mesh=mesh, in_specs=in_specs, out_specs=out_specs, check_vma=False
    )
```

```python
import functools
import math

import jax
import jax.numpy as jnp
from jax import lax
from jax.experimental import pallas as pl
from jax.experimental.pallas import tpu as pltpu
from jax.sharding import PartitionSpec as P

HEADS = 8
LANES = 128
GROUP = 2
PIECES = 2
AHEAD = 3
MESH = pl.DeviceIdType.MESH
F32 = jnp.float32
BF16 = jnp.bfloat16


def bit_count(size):
    return size.bit_length() - 1


PATHS = (
    "yxzm", "zmxy", "xyzm", "xzym", "yzxm", "zyxm", "zxym", "yxzm", "xyzm",
)
PLAN = (
    (0, -1), (1, -1), (2, -1), (3, -1), (4, -1), (5, -1), (6, -1), (7, -1), (8, -1),
    (0, 0), (1, 0), (2, 0), (4, 0), (3, 0), (7, 0), (5, 0), (6, 0), (8, 0),
    (0, 1), (2, 1), (1, 1), (7, 1), (5, 1), (6, 1), (8, 1), (4, 1), (3, 1),
    (0, 2), (1, 2), (5, 2), (2, 2), (6, 2), (4, 2), (3, 2), (7, 2), (1, 3),
    (8, 2), (5, 3), (6, 3), (4, 3), (3, 3),
)


def orders_of(frames_n, tiles_n):
    tile_bits = [("tile", b) for b in range(bit_count(GROUP), bit_count(tiles_n))]
    kinds = {
        "x": [("frame", b) for b in range(bit_count(frames_n))],
        "y": tile_bits[:1],
        "z": tile_bits[1:2],
        "m": tile_bits[2:],
    }
    return [sum((kinds[kind] for kind in path), []) for path in PATHS]


def plan_of(chunks, halvings):
    if chunks == len(PATHS) and halvings == len(PATHS[0]):
        return PLAN
    return [
        (k, stage)
        for stage in range(-1, halvings)
        for k in range(chunks)
        if stage < stages_of(k, halvings)
    ]


def ends_together(k):
    return PATHS[k % len(PATHS)].endswith("zm")


def stages_of(k, halvings):
    return halvings - 1 if ends_together(k) else halvings


def attend(queries, keys, values, own, wo, same_head):
    pixels, channels = queries[0].shape
    groups = channels // LANES
    scale = 1.0 / math.sqrt(channels // HEADS)
    heads_out = []
    for q in queries:
        wide = q.astype(F32)
        folded = []
        for k in keys:
            product = wide * k.astype(F32)
            total = product[:, :LANES]
            for c in range(1, groups):
                total = total + product[:, c * LANES : (c + 1) * LANES]
            high = total.astype(BF16)
            low = (total - high.astype(F32)).astype(BF16)
            folded.append(jnp.concatenate([high, low], axis=1))
        scores = jnp.dot(jnp.concatenate(folded, axis=0), same_head, preferred_element_type=F32)
        scores = [scores[g * pixels : (g + 1) * pixels] * scale for g in range(len(keys))]
        top = functools.reduce(jnp.maximum, scores)
        exps = [jnp.exp(s - top) for s in scores]
        share = 1.0 / functools.reduce(jnp.add, exps)
        acc = [None] * groups
        for e, v in zip(exps, values):
            weight = (e * share).astype(BF16).astype(F32)
            for c in range(groups):
                term = weight * v[:, c * LANES : (c + 1) * LANES].astype(F32)
                acc[c] = term if acc[c] is None else acc[c] + term
        heads_out.append(jnp.concatenate(acc, axis=1).astype(BF16))
    projected = jnp.dot(jnp.concatenate(heads_out, axis=0), wo, preferred_element_type=F32)
    return (own.astype(F32) + projected).astype(BF16)


def block_kernel(
    lat_hbm, conv_hbm, bias_ref, wq_hbm, wk_hbm, wv_hbm, wo_hbm, cot_hbm,
    mixed_hbm, grad_ref,
    lat_ref, conv_ref, weights, cot_ref, lat_rim, moved, hidden, others, queries, keys, values,
    turned, gathered, shifted, mixed_all, acc, part, recv,
    load_sem, conv_sem, own_sem, store_sem, rim_send, rim_recv, hid_send, hid_recv,
    cot_send, cot_recv, edge_send, edge_recv, mix_send, mix_recv, red_send, red_recv,
):
    frames, rows, cols, channels = lat_hbm.shape
    side = conv_hbm.shape[0]
    count, tiles = lax.axis_size("frame"), lax.axis_size("tile")
    frame, tile = lax.axis_index("frame"), lax.axis_index("tile")
    depth = tiles // GROUP
    block_rows = turned.shape[3]
    outs = depth * block_rows
    strip, member = tile // GROUP, lax.rem(tile, GROUP)
    has = (tile > 0, tile < tiles - 1)
    width = channels // count
    chunks, blocks = part.shape[0], part.shape[1]
    piece_cols = cols // PIECES

    squares = (wq_hbm, wk_hbm, wv_hbm, wo_hbm)
    lat_load = pltpu.make_async_copy(lat_hbm, lat_ref, load_sem.at[0])
    cot_load = pltpu.make_async_copy(cot_hbm, cot_ref, load_sem.at[1])
    taps = [(r, s) for r in range(side) for s in range(side)]
    conv_loads = [
        pltpu.make_async_copy(conv_hbm.at[r, s], conv_ref.at[r, s], conv_sem.at[r, s]) for r, s in taps
    ]
    square_loads = [
        pltpu.make_async_copy(source, weights.at[j], load_sem.at[2 + j])
        for j, source in enumerate(squares)
    ]
    for load in [lat_load] + conv_loads[:AHEAD]:
        load.start()

    def flip(axis, b):
        here = {"tile": tile, "frame": frame}[axis]
        return {axis: here + (1 - 2 * lax.rem(here // (1 << b), 2)) * (1 << b)}

    last_bits = range(bit_count(tiles) - 2, bit_count(tiles))

    def turned_by(bits, mask):
        return {"tile": tile + sum(flip("tile", b)["tile"] - tile for j, b in enumerate(bits) if (mask >> j) & 1)}

    barrier = pltpu.get_barrier_semaphore()

    def greet(friend):
        pl.semaphore_signal(barrier, inc=1, device_id=friend, device_id_type=MESH)

    for k in range(1, GROUP + 1):

        @pl.when(tile >= k)
        def _():
            greet({"tile": tile - k})

        @pl.when(tile < tiles - k)
        def _():
            greet({"tile": tile + k})

    greeted = [flip("tile", b) for b in range(bit_count(GROUP) + 1, bit_count(tiles))]
    greeted += [turned_by(last_bits, 3)]
    greeted += [{"frame": lax.rem(frame + k, count)} for k in range(1, count)]
    for friend in greeted:
        greet(friend)
    expected = jnp.minimum(tile, GROUP) + jnp.minimum(tiles - 1 - tile, GROUP) + len(greeted)

    def rim_copy(end, landed):
        return pltpu.make_async_remote_copy(
            src_ref=lat_hbm.at[:, (rows - 1) * end],
            dst_ref=lat_rim.at[end if landed else 1 - end],
            send_sem=rim_send.at[end],
            recv_sem=rim_recv.at[end if landed else 1 - end],
            device_id={"tile": tile + (1 if end else -1)},
            device_id_type=MESH,
        )

    def by_lead(value, offset, axis):
        if offset == 0:
            return value
        wide = value.astype(F32)
        rolled = pltpu.roll(wide, (-offset) % cols, axis)
        at = lax.broadcasted_iota(jnp.int32, wide.shape, axis)
        edge = 0 if offset < 0 else cols - 1
        return jnp.where(at == edge, 0.0, rolled).astype(BF16)

    def place(value, f, row):
        for s in range(side):
            moved[s, f, row] = by_lead(value, s - 1, 0)

    def cot_copy(k, landed):
        other = lax.rem(member + (GROUP - k if landed else k), GROUP)
        sender = other if landed else member
        return pltpu.make_async_remote_copy(
            src_ref=turned.at[:, :, other],
            dst_ref=gathered.at[:, :, :, pl.ds(pl.multiple_of(cols + sender * (rows * cols), LANES), rows * cols)],
            send_sem=cot_send.at[k - 1],
            recv_sem=cot_recv.at[k - 1],
            device_id={"tile": strip * GROUP + other},
            device_id_type=MESH,
        )

    def edge_copy(end, m):
        first = (rows - 1) * cols if end else 0
        target = 0 if end else (GROUP * rows + 1) * cols
        return pltpu.make_async_remote_copy(
            src_ref=turned.at[:, :, m, :, pl.ds(first, cols)],
            dst_ref=gathered.at[:, :, :, pl.ds(target, cols)],
            send_sem=edge_send.at[end, m],
            recv_sem=edge_recv.at[end],
            device_id={"tile": (strip + (1 if end else -1)) * GROUP + m},
            device_id_type=MESH,
        )

    edge_sends = (
        jnp.logical_and(member == 0, strip > 0),
        jnp.logical_and(member == GROUP - 1, strip < depth - 1),
    )
    own_cot = pltpu.make_async_copy(
        turned.at[:, :, member],
        gathered.at[:, :, :, pl.ds(pl.multiple_of(cols + member * (rows * cols), LANES), rows * cols)],
        own_sem.at[0],
    )
    lat_load.wait()
    for row in range(rows):
        for f in range(frames):
            place(lat_ref[f, row], f, row + 1)

    pl.semaphore_wait(barrier, expected)
    for end in range(2):

        @pl.when(has[end])
        def _():
            rim_copy(end, False).start()

    def hidden_copy(k, row, h):
        span = pl.ds(h * piece_cols, piece_cols)
        return pltpu.make_async_remote_copy(
            src_ref=hidden.at[row, :, span],
            dst_ref=others.at[k - 1, row, :, span],
            send_sem=hid_send.at[k - 1, row, h],
            recv_sem=hid_recv.at[k - 1, row, h],
            device_id={"frame": lax.rem(frame + k, count)},
            device_id_type=MESH,
        )

    def convolve(wanted, first):
        total = jnp.broadcast_to(bias_ref[...], (len(wanted) * frames * cols, channels))
        for t, (r, s) in enumerate(taps):
            if first:
                conv_loads[t].wait()
                if t + AHEAD < len(taps):
                    conv_loads[t + AHEAD].start()
            strips = [moved[s, :, row + r].reshape(frames * cols, channels) for row in wanted]
            total = total + jnp.dot(
                jnp.concatenate(strips, axis=0), conv_ref[r, s], preferred_element_type=F32
            )
        result = (total / (1.0 + jnp.exp(-total))).astype(BF16)
        for n, row in enumerate(wanted):
            part_of = result[n * frames * cols : (n + 1) * frames * cols]
            hidden[row] = part_of.reshape(frames, cols, channels)

    order = list(range(1, rows - 1)) + [rows - 1, 0]
    units = [(row, h) for row in order for h in range(PIECES)]

    def release(n):
        for k in range(1, count):
            hidden_copy(k, *units[n]).start()

    convolve(order[: rows - 2], True)
    for load in [cot_load] + square_loads:
        load.start()
    for n in range(2 * (rows - 2)):
        release(n)

    for load in square_loads:
        load.wait()
    head_dim = channels // HEADS
    i = lax.broadcasted_iota(jnp.int32, (channels, channels), 0)
    j = lax.broadcasted_iota(jnp.int32, (channels, channels), 1)
    spread = (i == lax.rem(j, HEADS) * head_dim + j // HEADS).astype(F32).astype(BF16)
    collect = (j == lax.rem(i, HEADS) * head_dim + i // HEADS).astype(F32).astype(BF16)
    for n in range(3):
        weights[n] = jnp.dot(weights[n], spread, preferred_element_type=F32).astype(BF16)
    weights[3] = jnp.dot(collect, weights[3], preferred_element_type=F32).astype(BF16)
    def project(row):
        tokens = hidden[row].reshape(frames * cols, channels)
        for n, target in enumerate((queries, keys, values)):
            result = jnp.dot(tokens, weights[n], preferred_element_type=F32)
            target[row] = result.astype(BF16).reshape(frames, cols, channels)

    for row in order[: rows - 2]:
        project(row)
    cot_load.wait()
    for f in range(frames):
        for row in range(rows):
            upright = cot_ref[f, row].T
            for d in range(depth):
                for m in range(GROUP):
                    at = (d * GROUP + m) * block_rows
                    turned[f, d, m, :, row * cols : (row + 1) * cols] = upright[at : at + block_rows]
    own_cot.start()
    for k in range(1, GROUP):
        cot_copy(k, False).start()
    for end in range(2):

        @pl.when(edge_sends[end])
        def _():
            for m in range(GROUP):
                edge_copy(end, m).start()

    for end in range(2):

        @pl.when(has[end])
        def _():
            rim_copy(end, True).wait_recv()

        @pl.when(jnp.logical_not(has[end]))
        def _():
            lat_rim[end] = jnp.zeros_like(lat_rim[end])

    for f in range(frames):
        place(lat_rim[0, f], f, 0)
        place(lat_rim[1, f], f, rows + 1)
    convolve(order[rows - 2 :], False)
    released = 2 * (rows - 2) + 1
    release(released - 1)
    for row in order[rows - 2 :]:
        project(row)

    own_cot.wait()
    for k in range(1, GROUP):
        cot_copy(k, True).wait_recv()
    rims = (strip > 0, strip < depth - 1)
    for end in range(2):
        target = 0 if end == 0 else (GROUP * rows + 1) * cols

        @pl.when(rims[end])
        def _():
            edge_copy(1 - end, 0).wait_recv()

        @pl.when(jnp.logical_not(rims[end]))
        def _():
            gathered[:, :, :, target : target + cols] = jnp.zeros(
                (frames, depth, block_rows, cols), BF16
            )

    for f in range(frames):
        for q in range(GROUP * rows + 2):
            value = gathered[f, :, :, q * cols : (q + 1) * cols].reshape(outs, cols)
            for s in range(side):
                shifted[f, s * outs : (s + 1) * outs, q * cols : (q + 1) * cols] = by_lead(value, 1 - s, 1)

    lane_i = lax.broadcasted_iota(jnp.int32, (2 * LANES, LANES), 0)
    lane_j = lax.broadcasted_iota(jnp.int32, (2 * LANES, LANES), 1)
    same_head = (lax.rem(lane_i, HEADS) == lax.rem(lane_j, HEADS)).astype(F32).astype(BF16)

    def mix_copy(row, h, landed):
        span = pl.ds(h * piece_cols, piece_cols)
        at = 1 - member if landed else member
        return pltpu.make_async_remote_copy(
            src_ref=mixed_all.at[row, member, :, span],
            dst_ref=mixed_all.at[row, at, :, span],
            send_sem=mix_send.at[row, h],
            recv_sem=mix_recv.at[row, h],
            device_id={"tile": strip * GROUP + 1 - member},
            device_id_type=MESH,
        )

    def attend_piece(row, h, following):
        span = pl.ds(h * piece_cols, piece_cols)
        for k in range(1, count):
            hidden_copy(k, row, h).wait_recv()
        if released <= following < len(units):
            release(following)
        own_k, own_v = [], []
        for f in range(frames):
            own_k.append(keys[row, f, span])
            own_v.append(values[row, f, span])
        for k in range(1, count):
            tokens = others[k - 1, row, :, span].reshape(frames * piece_cols, channels)
            kk = jnp.dot(tokens, weights[1], preferred_element_type=F32).astype(BF16)
            vv = jnp.dot(tokens, weights[2], preferred_element_type=F32).astype(BF16)
            for f in range(frames):
                own_k.append(kk[f * piece_cols : (f + 1) * piece_cols])
                own_v.append(vv[f * piece_cols : (f + 1) * piece_cols])
        mixed = attend(
            [queries[row, f, span] for f in range(frames)], own_k, own_v,
            hidden[row, :, span].reshape(frames * piece_cols, channels), weights[3], same_head,
        )
        mixed_all[row, member, :, span] = mixed.reshape(frames, piece_cols, channels)
        mix_copy(row, h, False).start()

    def store(row):
        return pltpu.make_async_copy(
            mixed_all.at[row, member], mixed_hbm.at[:, pl.ds(row * cols, cols)], store_sem.at[row]
        )

    def accumulate(row, first):
        for h in range(PIECES):
            mix_copy(row, h, True).wait_recv()
        maps = mixed_all[row].reshape(GROUP * frames * cols, channels)
        for r in range(side):
            spans = []
            for m in range(GROUP):
                lo = (m * rows + row + side - 1 - r) * cols
                for f in range(frames):
                    spans.append(shifted[f, :, lo : lo + cols])
            term = jnp.dot(jnp.concatenate(spans, axis=1), maps, preferred_element_type=F32)
            acc[r] = term if first else acc[r] + term

    for n, (row, h) in enumerate(units):
        attend_piece(row, h, n + 2)
        if h == PIECES - 1:
            store(row).start()
        if n >= PIECES + 1 and h == 1 % PIECES:
            accumulate(units[n - PIECES][0], n - PIECES < PIECES)
    accumulate(units[-1][0], len(units) == PIECES)

    orders = orders_of(count, tiles)
    halvings = len(orders[0])
    here = {"tile": tile, "frame": frame}

    def my_bit(axis, b):
        return lax.rem(here[axis] // (1 << b), 2)

    def order_of(k):
        return orders[k % len(orders)]

    def start_of(k, stage):
        total = 0
        for j in range(stage):
            total = total + my_bit(*order_of(k)[j]) * (blocks >> (j + 1))
        return total

    def last_place(mask):
        low, high = (my_bit("tile", b) for b in last_bits)
        low = 1 - low if mask & 1 else low
        high = 1 - high if mask & 2 else high
        return 2 * low + high

    def sum_copies(k, stage):
        todo = []
        if ends_together(k) and stage == halvings - 2:
            base = start_of(k, stage)
            for mask in range(1, 4):
                todo.append((base + last_place(mask), 1, mask, stage + mask - 1, turned_by(last_bits, mask)))
        else:
            axis, b = order_of(k)[stage]
            size = blocks >> (stage + 1)
            source = start_of(k, stage) + (1 - my_bit(axis, b)) * size
            todo.append((source, size, size, stage, flip(axis, b)))
        return [
            pltpu.make_async_remote_copy(
                src_ref=part.at[k, pl.ds(source, size)],
                dst_ref=recv.at[k, pl.ds(target, size)],
                send_sem=red_send.at[k, sem],
                recv_sem=red_recv.at[k, sem],
                device_id=device,
                device_id_type=MESH,
            )
            for source, size, target, sem, device in todo
        ]

    def cut(k):
        for f in range(count):
            unit = f * chunks + k
            tap, col = (unit * width) // channels, (unit * width) % channels
            r, s = tap // side, tap % side
            for d in range(depth):
                at = {"tile": d * GROUP, "frame": f}
                place_at = 0
                for j, (axis, b) in enumerate(order_of(k)):
                    place_at += ((at[axis] >> b) & 1) * (blocks >> (j + 1))
                lo = s * outs + d * block_rows
                part[k, place_at] = acc[r, lo : lo + block_rows, col : col + width].astype(BF16)
        for copy in sum_copies(k, 0):
            copy.start()

    def merge(k, stage):
        for copy in sum_copies(k, stage):
            copy.wait_recv()
        if ends_together(k) and stage == halvings - 2:
            total = part[k, start_of(k, stage) + last_place(0)].astype(F32)
            for mask in range(1, 4):
                total = total + recv[k, mask].astype(F32)
            grad_ref[:, k * width : (k + 1) * width] = total
            return
        size = blocks >> (stage + 1)
        mine = start_of(k, stage + 1)
        total = part[k, pl.ds(mine, size)].astype(F32) + recv[k, size : 2 * size].astype(F32)
        if stage < halvings - 1:
            part[k, pl.ds(mine, size)] = total.astype(BF16)
            for copy in sum_copies(k, stage + 1):
                copy.start()
        else:
            grad_ref[:, k * width : (k + 1) * width] = total[0]

    for k, stage in plan_of(chunks, halvings):
        if stage < 0:
            cut(k)
        else:
            merge(k, stage)

    for k in range(chunks):
        for stage in range(stages_of(k, halvings)):
            for copy in sum_copies(k, stage):
                copy.wait_send()
    for row, h in units:
        mix_copy(row, h, False).wait_send()
        for k in range(1, count):
            hidden_copy(k, row, h).wait_send()
    for row in range(rows):
        store(row).wait()
    for k in range(1, GROUP):
        cot_copy(k, False).wait_send()
    for end in range(2):

        @pl.when(has[end])
        def _():
            rim_copy(end, False).wait_send()

        @pl.when(edge_sends[end])
        def _():
            for m in range(GROUP):
                edge_copy(end, m).wait_send()


def block(latents, conv_weight, conv_bias, wq, wk, wv, wo, cotangent):
    frames, rows, cols, channels = latents.shape
    side = conv_weight.shape[0]
    out_channels = cotangent.shape[3]
    count, tiles = lax.axis_size("frame"), lax.axis_size("tile")
    chunks, width = side * side, channels // count
    depth, block_rows = tiles // GROUP, out_channels // tiles
    outs, blocks = depth * block_rows, count * depth
    stages = len(orders_of(count, tiles)[0]) + 1
    hbm = pl.BlockSpec(memory_space=pltpu.HBM)
    vmem = pl.BlockSpec(memory_space=pltpu.VMEM)
    maps = (rows, frames, cols, channels)
    dma = pltpu.SemaphoreType.DMA
    return pl.pallas_call(
        block_kernel,
        out_shape=[
            jax.ShapeDtypeStruct((frames, rows * cols, channels), BF16),
            jax.ShapeDtypeStruct((block_rows, chunks * width), F32),
        ],
        in_specs=[hbm, hbm, vmem] + [hbm] * 5,
        out_specs=[hbm, vmem],
        scratch_shapes=[
            pltpu.VMEM(latents.shape, BF16),
            pltpu.VMEM(conv_weight.shape, BF16),
            pltpu.VMEM((4, channels, channels), BF16),
            pltpu.VMEM(cotangent.shape, BF16),
            pltpu.VMEM((2, frames, cols, channels), BF16),
            pltpu.VMEM((side, frames, rows + 2, cols, channels), BF16),
            pltpu.VMEM(maps, BF16),
            pltpu.VMEM((count - 1,) + maps, BF16),
            pltpu.VMEM(maps, BF16),
            pltpu.VMEM(maps, BF16),
            pltpu.VMEM(maps, BF16),
            pltpu.VMEM((frames, depth, GROUP, block_rows, rows * cols), BF16),
            pltpu.VMEM((frames, depth, block_rows, (GROUP * rows + 2) * cols), BF16),
            pltpu.VMEM((frames, side * outs, (GROUP * rows + 2) * cols), BF16),
            pltpu.VMEM((rows, GROUP, frames, cols, channels), BF16),
            pltpu.VMEM((side, side * outs, channels), F32),
            pltpu.VMEM((chunks, blocks, block_rows, width), BF16),
            pltpu.VMEM((chunks, blocks, block_rows, width), BF16),
            dma((6,)),
            dma((side, side)),
            dma((1,)),
            dma((rows,)),
            dma((2,)),
            dma((2,)),
            dma((count - 1, rows, PIECES)),
            dma((count - 1, rows, PIECES)),
            dma((GROUP - 1,)),
            dma((GROUP - 1,)),
            dma((2, GROUP)),
            dma((2,)),
            dma((rows, PIECES)),
            dma((rows, PIECES)),
            dma((chunks, stages)),
            dma((chunks, stages)),
        ],
        compiler_params=pltpu.CompilerParams(
            collective_id=0, has_side_effects=True, vmem_limit_bytes=63 * 1024 * 1024
        ),
    )(latents, conv_weight, conv_bias.reshape(1, -1), wq, wk, wv, wo, cotangent)


def settle_kernel(mixed_in, grad_in, mixed_out, grad_out, mixed_held, grad_held, in_sem, out_sem):
    half = mixed_in.shape[1] // 2
    parts = [(grad_in, grad_held, grad_out)]
    for f in range(mixed_in.shape[0]):
        for h in range(2):
            at = (f, pl.ds(h * half, half))
            parts.append((mixed_in.at[at], mixed_held.at[at], mixed_out.at[at]))
    inward = [pltpu.make_async_copy(a, b, in_sem.at[n]) for n, (a, b, _) in enumerate(parts)]
    outward = [pltpu.make_async_copy(b, c, out_sem.at[n]) for n, (_, b, c) in enumerate(parts)]
    for copy in inward:
        copy.start()
    for first, second in zip(inward, outward):
        first.wait()
        second.start()
    for copy in outward:
        copy.wait()


def settled(mixed, grad):
    hbm = pl.BlockSpec(memory_space=pltpu.HBM)
    parts = 1 + 2 * mixed.shape[0]
    return pl.pallas_call(
        settle_kernel,
        out_shape=[
            jax.ShapeDtypeStruct(mixed.shape, mixed.dtype),
            jax.ShapeDtypeStruct(grad.shape, grad.dtype),
        ],
        in_specs=[hbm, hbm],
        out_specs=[hbm, hbm],
        scratch_shapes=[
            pltpu.VMEM(mixed.shape, mixed.dtype),
            pltpu.VMEM(grad.shape, grad.dtype),
            pltpu.SemaphoreType.DMA((parts,)),
            pltpu.SemaphoreType.DMA((parts,)),
        ],
    )(mixed, grad)


def on_device(
    latents, conv_weight, conv_bias, query_weight, key_weight, value_weight, out_weight, cotangent
):
    frames, rows, cols, channels = latents.shape
    mixed, conv_grad = settled(
        *block(
            latents, conv_weight, conv_bias, query_weight, key_weight, value_weight, out_weight, cotangent
        )
    )
    return (mixed.reshape(frames, rows, cols, channels), conv_grad)


def solution(mesh):
    in_specs = (
        P("frame", "tile", None, None),
        P(),
        P(),
        P(),
        P(),
        P(),
        P(),
        P("frame", "tile", None, None),
    )
    out_specs = (P("frame", "tile", None, None), P("tile", "frame"))
    return jax.shard_map(
        on_device, mesh=mesh, in_specs=in_specs, out_specs=out_specs, check_vma=False
    )
```

```python
import functools
import math

import jax
import jax.numpy as jnp
from jax import lax
from jax.experimental import pallas as pl
from jax.experimental.pallas import tpu as pltpu
from jax.sharding import PartitionSpec as P

HEADS = 8
LANES = 128
GROUP = 2
PIECES = 2
AHEAD = 3
MESH = pl.DeviceIdType.MESH
F32 = jnp.float32
BF16 = jnp.bfloat16


def bit_count(size):
    return size.bit_length() - 1


PATHS = (
    "yxzm", "zmxy", "xyzm", "xzym", "yzxm", "zyxm", "zxym", "yxzm", "xyzm",
)
PLAN = (
    (0, -1), (1, -1), (2, -1), (3, -1), (4, -1), (5, -1), (6, -1), (7, -1), (8, -1),
    (0, 0), (1, 0), (2, 0), (4, 0), (3, 0), (7, 0), (5, 0), (6, 0), (8, 0),
    (0, 1), (2, 1), (1, 1), (7, 1), (5, 1), (6, 1), (8, 1), (4, 1), (3, 1),
    (0, 2), (1, 2), (5, 2), (2, 2), (6, 2), (4, 2), (3, 2), (7, 2), (1, 3),
    (8, 2), (5, 3), (6, 3), (4, 3), (3, 3),
)


def orders_of(frames_n, tiles_n):
    tile_bits = [("tile", b) for b in range(bit_count(GROUP), bit_count(tiles_n))]
    kinds = {
        "x": [("frame", b) for b in range(bit_count(frames_n))],
        "y": tile_bits[:1],
        "z": tile_bits[1:2],
        "m": tile_bits[2:],
    }
    return [sum((kinds[kind] for kind in path), []) for path in PATHS]


def plan_of(chunks, halvings):
    if chunks == len(PATHS) and halvings == len(PATHS[0]):
        return PLAN
    return [
        (k, stage)
        for stage in range(-1, halvings)
        for k in range(chunks)
        if stage < stages_of(k, halvings)
    ]


def ends_together(k):
    return PATHS[k % len(PATHS)].endswith("zm")


def stages_of(k, halvings):
    return halvings - 1 if ends_together(k) else halvings


def attend(queries, keys, values, own, wo, same_head):
    pixels, channels = queries[0].shape
    groups = channels // LANES
    scale = 1.0 / math.sqrt(channels // HEADS)
    heads_out = []
    for q in queries:
        wide = q.astype(F32)
        folded = []
        for k in keys:
            product = wide * k.astype(F32)
            total = product[:, :LANES]
            for c in range(1, groups):
                total = total + product[:, c * LANES : (c + 1) * LANES]
            high = total.astype(BF16)
            low = (total - high.astype(F32)).astype(BF16)
            folded.append(jnp.concatenate([high, low], axis=1))
        scores = jnp.dot(jnp.concatenate(folded, axis=0), same_head, preferred_element_type=F32)
        scores = [scores[g * pixels : (g + 1) * pixels] * scale for g in range(len(keys))]
        top = functools.reduce(jnp.maximum, scores)
        exps = [jnp.exp(s - top) for s in scores]
        share = 1.0 / functools.reduce(jnp.add, exps)
        acc = [None] * groups
        for e, v in zip(exps, values):
            weight = (e * share).astype(BF16).astype(F32)
            for c in range(groups):
                term = weight * v[:, c * LANES : (c + 1) * LANES].astype(F32)
                acc[c] = term if acc[c] is None else acc[c] + term
        heads_out.append(jnp.concatenate(acc, axis=1).astype(BF16))
    projected = jnp.dot(jnp.concatenate(heads_out, axis=0), wo, preferred_element_type=F32)
    return (own.astype(F32) + projected).astype(BF16)


def block_kernel(
    lat_hbm, conv_hbm, bias_ref, wq_hbm, wk_hbm, wv_hbm, wo_hbm, cot_hbm,
    mixed_hbm, grad_ref,
    lat_ref, conv_ref, weights, cot_ref, lat_rim, moved, hidden, others, queries, keys, values,
    turned, gathered, shifted, mixed_all, acc, part, recv,
    load_sem, conv_sem, own_sem, store_sem, rim_send, rim_recv, hid_send, hid_recv,
    cot_send, cot_recv, edge_send, edge_recv, mix_send, mix_recv, red_send, red_recv,
):
    frames, rows, cols, channels = lat_hbm.shape
    side = conv_hbm.shape[0]
    count, tiles = lax.axis_size("frame"), lax.axis_size("tile")
    frame, tile = lax.axis_index("frame"), lax.axis_index("tile")
    depth = tiles // GROUP
    block_rows = turned.shape[3]
    outs = depth * block_rows
    strip, member = tile // GROUP, lax.rem(tile, GROUP)
    has = (tile > 0, tile < tiles - 1)
    width = channels // count
    chunks, blocks = part.shape[0], part.shape[1]
    piece_cols = cols // PIECES

    squares = (wq_hbm, wk_hbm, wv_hbm, wo_hbm)
    lat_load = pltpu.make_async_copy(lat_hbm, lat_ref, load_sem.at[0])
    cot_load = pltpu.make_async_copy(cot_hbm, cot_ref, load_sem.at[1])
    taps = [(r, s) for r in range(side) for s in range(side)]
    conv_loads = [
        pltpu.make_async_copy(conv_hbm.at[r, s], conv_ref.at[r, s], conv_sem.at[r, s]) for r, s in taps
    ]
    square_loads = [
        pltpu.make_async_copy(source, weights.at[j], load_sem.at[2 + j])
        for j, source in enumerate(squares)
    ]
    for load in [lat_load] + conv_loads[:AHEAD]:
        load.start()

    def flip(axis, b):
        here = {"tile": tile, "frame": frame}[axis]
        return {axis: here + (1 - 2 * lax.rem(here // (1 << b), 2)) * (1 << b)}

    last_bits = range(bit_count(tiles) - 2, bit_count(tiles))

    def turned_by(bits, mask):
        return {"tile": tile + sum(flip("tile", b)["tile"] - tile for j, b in enumerate(bits) if (mask >> j) & 1)}

    barrier = pltpu.get_barrier_semaphore()

    def greet(friend):
        pl.semaphore_signal(barrier, inc=1, device_id=friend, device_id_type=MESH)

    for k in range(1, GROUP + 1):

        @pl.when(tile >= k)
        def _():
            greet({"tile": tile - k})

        @pl.when(tile < tiles - k)
        def _():
            greet({"tile": tile + k})

    greeted = [flip("tile", b) for b in range(bit_count(GROUP) + 1, bit_count(tiles))]
    greeted += [turned_by(last_bits, 3)]
    greeted += [{"frame": lax.rem(frame + k, count)} for k in range(1, count)]
    for friend in greeted:
        greet(friend)
    expected = jnp.minimum(tile, GROUP) + jnp.minimum(tiles - 1 - tile, GROUP) + len(greeted)

    def rim_copy(end, landed):
        return pltpu.make_async_remote_copy(
            src_ref=lat_hbm.at[:, (rows - 1) * end],
            dst_ref=lat_rim.at[end if landed else 1 - end],
            send_sem=rim_send.at[end],
            recv_sem=rim_recv.at[end if landed else 1 - end],
            device_id={"tile": tile + (1 if end else -1)},
            device_id_type=MESH,
        )

    def by_lead(value, offset, axis):
        if offset == 0:
            return value
        wide = value.astype(F32)
        rolled = pltpu.roll(wide, (-offset) % cols, axis)
        at = lax.broadcasted_iota(jnp.int32, wide.shape, axis)
        edge = 0 if offset < 0 else cols - 1
        return jnp.where(at == edge, 0.0, rolled).astype(BF16)

    def place(value, f, row):
        for s in range(side):
            moved[s, f, row] = by_lead(value, s - 1, 0)

    def cot_copy(k, landed):
        other = lax.rem(member + (GROUP - k if landed else k), GROUP)
        sender = other if landed else member
        return pltpu.make_async_remote_copy(
            src_ref=turned.at[:, :, other],
            dst_ref=gathered.at[:, :, :, pl.ds(pl.multiple_of(cols + sender * (rows * cols), LANES), rows * cols)],
            send_sem=cot_send.at[k - 1],
            recv_sem=cot_recv.at[k - 1],
            device_id={"tile": strip * GROUP + other},
            device_id_type=MESH,
        )

    def edge_copy(end, m):
        first = (rows - 1) * cols if end else 0
        target = 0 if end else (GROUP * rows + 1) * cols
        return pltpu.make_async_remote_copy(
            src_ref=turned.at[:, :, m, :, pl.ds(first, cols)],
            dst_ref=gathered.at[:, :, :, pl.ds(target, cols)],
            send_sem=edge_send.at[end, m],
            recv_sem=edge_recv.at[end],
            device_id={"tile": (strip + (1 if end else -1)) * GROUP + m},
            device_id_type=MESH,
        )

    edge_sends = (
        jnp.logical_and(member == 0, strip > 0),
        jnp.logical_and(member == GROUP - 1, strip < depth - 1),
    )
    own_cot = pltpu.make_async_copy(
        turned.at[:, :, member],
        gathered.at[:, :, :, pl.ds(pl.multiple_of(cols + member * (rows * cols), LANES), rows * cols)],
        own_sem.at[0],
    )
    lat_load.wait()
    for row in range(rows):
        for f in range(frames):
            place(lat_ref[f, row], f, row + 1)

    pl.semaphore_wait(barrier, expected)
    for end in range(2):

        @pl.when(has[end])
        def _():
            rim_copy(end, False).start()

    def hidden_copy(k, row, h):
        span = pl.ds(h * piece_cols, piece_cols)
        return pltpu.make_async_remote_copy(
            src_ref=hidden.at[row, :, span],
            dst_ref=others.at[k - 1, row, :, span],
            send_sem=hid_send.at[k - 1, row, h],
            recv_sem=hid_recv.at[k - 1, row, h],
            device_id={"frame": lax.rem(frame + k, count)},
            device_id_type=MESH,
        )

    def convolve(wanted, first):
        total = jnp.broadcast_to(bias_ref[...], (len(wanted) * frames * cols, channels))
        for t, (r, s) in enumerate(taps):
            if first:
                conv_loads[t].wait()
                if t + AHEAD < len(taps):
                    conv_loads[t + AHEAD].start()
            strips = [moved[s, :, row + r].reshape(frames * cols, channels) for row in wanted]
            total = total + jnp.dot(
                jnp.concatenate(strips, axis=0), conv_ref[r, s], preferred_element_type=F32
            )
        result = (total / (1.0 + jnp.exp(-total))).astype(BF16)
        for n, row in enumerate(wanted):
            part_of = result[n * frames * cols : (n + 1) * frames * cols]
            hidden[row] = part_of.reshape(frames, cols, channels)

    order = list(range(1, rows - 1)) + [rows - 1, 0]
    units = [(row, h) for row in order for h in range(PIECES)]

    def release(n):
        for k in range(1, count):
            hidden_copy(k, *units[n]).start()

    convolve(order[: rows - 2], True)
    for load in [cot_load] + square_loads:
        load.start()
    for n in range(2 * (rows - 2)):
        release(n)

    for load in square_loads:
        load.wait()
    head_dim = channels // HEADS
    i = lax.broadcasted_iota(jnp.int32, (channels, channels), 0)
    j = lax.broadcasted_iota(jnp.int32, (channels, channels), 1)
    spread = (i == lax.rem(j, HEADS) * head_dim + j // HEADS).astype(F32).astype(BF16)
    collect = (j == lax.rem(i, HEADS) * head_dim + i // HEADS).astype(F32).astype(BF16)
    for n in range(3):
        weights[n] = jnp.dot(weights[n], spread, preferred_element_type=F32).astype(BF16)
    weights[3] = jnp.dot(collect, weights[3], preferred_element_type=F32).astype(BF16)
    def project(row):
        tokens = hidden[row].reshape(frames * cols, channels)
        for n, target in enumerate((queries, keys, values)):
            result = jnp.dot(tokens, weights[n], preferred_element_type=F32)
            target[row] = result.astype(BF16).reshape(frames, cols, channels)

    for row in order[: rows - 2]:
        project(row)
    cot_load.wait()
    for f in range(frames):
        for row in range(rows):
            upright = cot_ref[f, row].T
            for d in range(depth):
                for m in range(GROUP):
                    at = (d * GROUP + m) * block_rows
                    turned[f, d, m, :, row * cols : (row + 1) * cols] = upright[at : at + block_rows]
    own_cot.start()
    for k in range(1, GROUP):
        cot_copy(k, False).start()
    for end in range(2):

        @pl.when(edge_sends[end])
        def _():
            for m in range(GROUP):
                edge_copy(end, m).start()

    for end in range(2):

        @pl.when(has[end])
        def _():
            rim_copy(end, True).wait_recv()

        @pl.when(jnp.logical_not(has[end]))
        def _():
            lat_rim[end] = jnp.zeros_like(lat_rim[end])

    for f in range(frames):
        place(lat_rim[0, f], f, 0)
        place(lat_rim[1, f], f, rows + 1)
    convolve(order[rows - 2 :], False)
    released = 2 * (rows - 2) + 1
    release(released - 1)
    for row in order[rows - 2 :]:
        project(row)

    own_cot.wait()
    for k in range(1, GROUP):
        cot_copy(k, True).wait_recv()
    rims = (strip > 0, strip < depth - 1)
    for end in range(2):
        target = 0 if end == 0 else (GROUP * rows + 1) * cols

        @pl.when(rims[end])
        def _():
            edge_copy(1 - end, 0).wait_recv()

        @pl.when(jnp.logical_not(rims[end]))
        def _():
            gathered[:, :, :, target : target + cols] = jnp.zeros(
                (frames, depth, block_rows, cols), BF16
            )

    for f in range(frames):
        for q in range(GROUP * rows + 2):
            value = gathered[f, :, :, q * cols : (q + 1) * cols].reshape(outs, cols)
            for s in range(side):
                shifted[f, s * outs : (s + 1) * outs, q * cols : (q + 1) * cols] = by_lead(value, 1 - s, 1)

    lane_i = lax.broadcasted_iota(jnp.int32, (2 * LANES, LANES), 0)
    lane_j = lax.broadcasted_iota(jnp.int32, (2 * LANES, LANES), 1)
    same_head = (lax.rem(lane_i, HEADS) == lax.rem(lane_j, HEADS)).astype(F32).astype(BF16)

    def mix_copy(row, h, landed):
        span = pl.ds(h * piece_cols, piece_cols)
        at = 1 - member if landed else member
        return pltpu.make_async_remote_copy(
            src_ref=mixed_all.at[row, member, :, span],
            dst_ref=mixed_all.at[row, at, :, span],
            send_sem=mix_send.at[row, h],
            recv_sem=mix_recv.at[row, h],
            device_id={"tile": strip * GROUP + 1 - member},
            device_id_type=MESH,
        )

    def attend_piece(row, h, following):
        span = pl.ds(h * piece_cols, piece_cols)
        for k in range(1, count):
            hidden_copy(k, row, h).wait_recv()
        if released <= following < len(units):
            release(following)
        own_k, own_v = [], []
        for f in range(frames):
            own_k.append(keys[row, f, span])
            own_v.append(values[row, f, span])
        for k in range(1, count):
            tokens = others[k - 1, row, :, span].reshape(frames * piece_cols, channels)
            kk = jnp.dot(tokens, weights[1], preferred_element_type=F32).astype(BF16)
            vv = jnp.dot(tokens, weights[2], preferred_element_type=F32).astype(BF16)
            for f in range(frames):
                own_k.append(kk[f * piece_cols : (f + 1) * piece_cols])
                own_v.append(vv[f * piece_cols : (f + 1) * piece_cols])
        mixed = attend(
            [queries[row, f, span] for f in range(frames)], own_k, own_v,
            hidden[row, :, span].reshape(frames * piece_cols, channels), weights[3], same_head,
        )
        mixed_all[row, member, :, span] = mixed.reshape(frames, piece_cols, channels)
        mix_copy(row, h, False).start()

    def store(row):
        return pltpu.make_async_copy(
            mixed_all.at[row, member], mixed_hbm.at[:, pl.ds(row * cols, cols)], store_sem.at[row]
        )

    def accumulate(row, first, after=lambda r: None):
        for h in range(PIECES):
            mix_copy(row, h, True).wait_recv()
        maps = mixed_all[row].reshape(GROUP * frames * cols, channels)
        for r in range(side):
            spans = []
            for m in range(GROUP):
                lo = (m * rows + row + side - 1 - r) * cols
                for f in range(frames):
                    spans.append(shifted[f, :, lo : lo + cols])
            term = jnp.dot(jnp.concatenate(spans, axis=1), maps, preferred_element_type=F32)
            acc[r] = term if first else acc[r] + term
            after(r)

    for n, (row, h) in enumerate(units):
        attend_piece(row, h, n + 2)
        if h == PIECES - 1:
            store(row).start()
        if n >= PIECES + 1 and h == 1 % PIECES:
            accumulate(units[n - PIECES][0], n - PIECES < PIECES)

    orders = orders_of(count, tiles)
    halvings = len(orders[0])
    here = {"tile": tile, "frame": frame}

    def my_bit(axis, b):
        return lax.rem(here[axis] // (1 << b), 2)

    def order_of(k):
        return orders[k % len(orders)]

    def start_of(k, stage):
        total = 0
        for j in range(stage):
            total = total + my_bit(*order_of(k)[j]) * (blocks >> (j + 1))
        return total

    def last_place(mask):
        low, high = (my_bit("tile", b) for b in last_bits)
        low = 1 - low if mask & 1 else low
        high = 1 - high if mask & 2 else high
        return 2 * low + high

    def sum_copies(k, stage):
        todo = []
        if ends_together(k) and stage == halvings - 2:
            base = start_of(k, stage)
            for mask in range(1, 4):
                todo.append((base + last_place(mask), 1, mask, stage + mask - 1, turned_by(last_bits, mask)))
        else:
            axis, b = order_of(k)[stage]
            size = blocks >> (stage + 1)
            source = start_of(k, stage) + (1 - my_bit(axis, b)) * size
            todo.append((source, size, size, stage, flip(axis, b)))
        return [
            pltpu.make_async_remote_copy(
                src_ref=part.at[k, pl.ds(source, size)],
                dst_ref=recv.at[k, pl.ds(target, size)],
                send_sem=red_send.at[k, sem],
                recv_sem=red_recv.at[k, sem],
                device_id=device,
                device_id_type=MESH,
            )
            for source, size, target, sem, device in todo
        ]

    def cut(k):
        for f in range(count):
            unit = f * chunks + k
            tap, col = (unit * width) // channels, (unit * width) % channels
            r, s = tap // side, tap % side
            for d in range(depth):
                at = {"tile": d * GROUP, "frame": f}
                place_at = 0
                for j, (axis, b) in enumerate(order_of(k)):
                    place_at += ((at[axis] >> b) & 1) * (blocks >> (j + 1))
                lo = s * outs + d * block_rows
                part[k, place_at] = acc[r, lo : lo + block_rows, col : col + width].astype(BF16)
        for copy in sum_copies(k, 0):
            copy.start()

    def merge(k, stage):
        for copy in sum_copies(k, stage):
            copy.wait_recv()
        if ends_together(k) and stage == halvings - 2:
            total = part[k, start_of(k, stage) + last_place(0)].astype(F32)
            for mask in range(1, 4):
                total = total + recv[k, mask].astype(F32)
            grad_ref[:, k * width : (k + 1) * width] = total
            return
        size = blocks >> (stage + 1)
        mine = start_of(k, stage + 1)
        total = part[k, pl.ds(mine, size)].astype(F32) + recv[k, size : 2 * size].astype(F32)
        if stage < halvings - 1:
            part[k, pl.ds(mine, size)] = total.astype(BF16)
            for copy in sum_copies(k, stage + 1):
                copy.start()
        else:
            grad_ref[:, k * width : (k + 1) * width] = total[0]

    def last_taps(k):
        return max((f * chunks + k) * width // channels // side for f in range(count))

    plan = plan_of(chunks, halvings)
    early = [k for k, stage in plan if stage < 0 and last_taps(k) < side - 1]

    def hand_out(r):
        for k in early:
            if last_taps(k) == r:
                cut(k)

    accumulate(units[-1][0], len(units) == PIECES, hand_out)
    for k, stage in plan:
        if stage < 0:
            if k not in early:
                cut(k)
        else:
            merge(k, stage)

    for k in range(chunks):
        for stage in range(stages_of(k, halvings)):
            for copy in sum_copies(k, stage):
                copy.wait_send()
    for row, h in units:
        mix_copy(row, h, False).wait_send()
        for k in range(1, count):
            hidden_copy(k, row, h).wait_send()
    for row in range(rows):
        store(row).wait()
    for k in range(1, GROUP):
        cot_copy(k, False).wait_send()
    for end in range(2):

        @pl.when(has[end])
        def _():
            rim_copy(end, False).wait_send()

        @pl.when(edge_sends[end])
        def _():
            for m in range(GROUP):
                edge_copy(end, m).wait_send()


def block(latents, conv_weight, conv_bias, wq, wk, wv, wo, cotangent):
    frames, rows, cols, channels = latents.shape
    side = conv_weight.shape[0]
    out_channels = cotangent.shape[3]
    count, tiles = lax.axis_size("frame"), lax.axis_size("tile")
    chunks, width = side * side, channels // count
    depth, block_rows = tiles // GROUP, out_channels // tiles
    outs, blocks = depth * block_rows, count * depth
    stages = len(orders_of(count, tiles)[0]) + 1
    hbm = pl.BlockSpec(memory_space=pltpu.HBM)
    vmem = pl.BlockSpec(memory_space=pltpu.VMEM)
    maps = (rows, frames, cols, channels)
    dma = pltpu.SemaphoreType.DMA
    return pl.pallas_call(
        block_kernel,
        out_shape=[
            jax.ShapeDtypeStruct((frames, rows * cols, channels), BF16),
            jax.ShapeDtypeStruct((block_rows, chunks * width), F32),
        ],
        in_specs=[hbm, hbm, vmem] + [hbm] * 5,
        out_specs=[hbm, vmem],
        scratch_shapes=[
            pltpu.VMEM(latents.shape, BF16),
            pltpu.VMEM(conv_weight.shape, BF16),
            pltpu.VMEM((4, channels, channels), BF16),
            pltpu.VMEM(cotangent.shape, BF16),
            pltpu.VMEM((2, frames, cols, channels), BF16),
            pltpu.VMEM((side, frames, rows + 2, cols, channels), BF16),
            pltpu.VMEM(maps, BF16),
            pltpu.VMEM((count - 1,) + maps, BF16),
            pltpu.VMEM(maps, BF16),
            pltpu.VMEM(maps, BF16),
            pltpu.VMEM(maps, BF16),
            pltpu.VMEM((frames, depth, GROUP, block_rows, rows * cols), BF16),
            pltpu.VMEM((frames, depth, block_rows, (GROUP * rows + 2) * cols), BF16),
            pltpu.VMEM((frames, side * outs, (GROUP * rows + 2) * cols), BF16),
            pltpu.VMEM((rows, GROUP, frames, cols, channels), BF16),
            pltpu.VMEM((side, side * outs, channels), F32),
            pltpu.VMEM((chunks, blocks, block_rows, width), BF16),
            pltpu.VMEM((chunks, blocks, block_rows, width), BF16),
            dma((6,)),
            dma((side, side)),
            dma((1,)),
            dma((rows,)),
            dma((2,)),
            dma((2,)),
            dma((count - 1, rows, PIECES)),
            dma((count - 1, rows, PIECES)),
            dma((GROUP - 1,)),
            dma((GROUP - 1,)),
            dma((2, GROUP)),
            dma((2,)),
            dma((rows, PIECES)),
            dma((rows, PIECES)),
            dma((chunks, stages)),
            dma((chunks, stages)),
        ],
        compiler_params=pltpu.CompilerParams(
            collective_id=0, has_side_effects=True, vmem_limit_bytes=63 * 1024 * 1024
        ),
    )(latents, conv_weight, conv_bias.reshape(1, -1), wq, wk, wv, wo, cotangent)


def settle_kernel(mixed_in, grad_in, mixed_out, grad_out, mixed_held, grad_held, in_sem, out_sem):
    half = mixed_in.shape[1] // 2
    parts = [(grad_in, grad_held, grad_out)]
    for f in range(mixed_in.shape[0]):
        for h in range(2):
            at = (f, pl.ds(h * half, half))
            parts.append((mixed_in.at[at], mixed_held.at[at], mixed_out.at[at]))
    inward = [pltpu.make_async_copy(a, b, in_sem.at[n]) for n, (a, b, _) in enumerate(parts)]
    outward = [pltpu.make_async_copy(b, c, out_sem.at[n]) for n, (_, b, c) in enumerate(parts)]
    for copy in inward:
        copy.start()
    for first, second in zip(inward, outward):
        first.wait()
        second.start()
    for copy in outward:
        copy.wait()


def settled(mixed, grad):
    hbm = pl.BlockSpec(memory_space=pltpu.HBM)
    parts = 1 + 2 * mixed.shape[0]
    return pl.pallas_call(
        settle_kernel,
        out_shape=[
            jax.ShapeDtypeStruct(mixed.shape, mixed.dtype),
            jax.ShapeDtypeStruct(grad.shape, grad.dtype),
        ],
        in_specs=[hbm, hbm],
        out_specs=[hbm, hbm],
        scratch_shapes=[
            pltpu.VMEM(mixed.shape, mixed.dtype),
            pltpu.VMEM(grad.shape, grad.dtype),
            pltpu.SemaphoreType.DMA((parts,)),
            pltpu.SemaphoreType.DMA((parts,)),
        ],
    )(mixed, grad)


def on_device(
    latents, conv_weight, conv_bias, query_weight, key_weight, value_weight, out_weight, cotangent
):
    frames, rows, cols, channels = latents.shape
    mixed, conv_grad = settled(
        *block(
            latents, conv_weight, conv_bias, query_weight, key_weight, value_weight, out_weight, cotangent
        )
    )
    return (mixed.reshape(frames, rows, cols, channels), conv_grad)


def solution(mesh):
    in_specs = (
        P("frame", "tile", None, None),
        P(),
        P(),
        P(),
        P(),
        P(),
        P(),
        P("frame", "tile", None, None),
    )
    out_specs = (P("frame", "tile", None, None), P("tile", "frame"))
    return jax.shard_map(
        on_device, mesh=mesh, in_specs=in_specs, out_specs=out_specs, check_vma=False
    )
```
